32 devices in a mesh: shot: 8 (over z, y), off: 4 (over x, core).
Axes of the slice: x: 2, y: 2, z: 4, core: 2. Of those that a mesh axis runs over, the one named last changes fastest.
Arguments:
- traces: bfloat16 [32, 768, 2048], P('shot', 'off'), may hold values from -60 to 60
- offset_bin: int32 [32, 768], P('shot', 'off'), may hold values from 0 to 31, as said below
- rec_id: int32 [32, 768], P('shot', 'off'), may hold values from 0 to 2047, as said below
- cmp_id: int32 [32, 768], P('shot', 'off'), may hold values from 0 to 4095, as said below
- rec_owner: int32 [2048], replicated, may hold values from 0 to 7, as said below
- rec_slot: int32 [2048], replicated, may hold values from 0 to 255
- cmp_owner: int32 [4096], replicated, may hold values from 0 to 7, as said below
- cmp_slot: int32 [4096], replicated, may hold values from 0 to 511
Outputs:
- source_term: float32 [32, 640], P('shot')
- offset_term: float32 [32, 640], P('off')
- receiver_term: float32 [2048, 640], P(('shot', 'off'))
- midpoint_term: float32 [4096, 640], P(('shot', 'off'))
The draws below stay inside these ranges and needn't reach their ends.
Inputs may be any that keep to these rules, and one draw needn't show every extreme that they name: `offset_bin`: a trace at position j of its shot has a bin of (j // 192) * 8 to (j // 192 + 1) * 8 - 1. rec_owner[r] * 256 + rec_slot[r] takes every value below 2048 exactly once. cmp_owner[c] * 512 + cmp_slot[c] takes every value below 4096 exactly once. `rec_id`: of the traces of one device's block (4 shots by 192 traces) at most 192 have receivers of any one owner; for every offset group some owner gets exactly 192 from every block of that group. `cmp_id`: of the traces of one device's block at most 192 have midpoints of any one owner; for every offset group some owner gets exactly 192 from every block of that group.
All inputs are finite; a program needn't handle non-finite values.
Results may differ from the reference program's by a relative error of at most 0.0035.
Values may be sent and summed in bfloat16 or wider, within the bound.
A program may use at most 64 MiB of HBM per device.

```python
import math
import jax
import jax.numpy as jnp
from jax import lax

NT = 2048
NF = 640
SHOT_DEV = 4
TR_OFF = 192
OFFB_DEV = 8
REC_DEV = 256
CMP_DEV = 512
SWEEPS = 2
SHOTS = 32
TR_SHOT = 768
NOFF = 32
NREC = 2048
NCMP = 4096
N_SHOT = 8
N_OFF = 4


def owner_tables(seed_key, count_dev):
    total_n = count_dev * N_SHOT
    shuffle = jax.random.permutation(seed_key, total_n).astype(jnp.int32)
    position = jnp.zeros((total_n,), jnp.int32).at[shuffle].set(jnp.arange(total_n, dtype=jnp.int32))
    return (position // count_dev, position % count_dev, shuffle)


def block_layout(values):
    shaped = values.reshape(N_SHOT, N_OFF, SHOT_DEV, TR_OFF)
    return jnp.transpose(shaped, (0, 2, 1, 3)).reshape(SHOTS, TR_SHOT)


def trace_ids(seed_key, count_dev):
    owners, places, shuffle = owner_tables(jax.random.fold_in(seed_key, 1), count_dev)
    per_dev = SHOT_DEV * TR_OFF
    capacity = 2 * per_dev // N_SHOT
    hottest = jax.random.randint(jax.random.fold_in(seed_key, 2), (1, N_OFF, 1), 0, N_SHOT)
    starting = jax.random.randint(jax.random.fold_in(seed_key, 3), (N_SHOT, N_OFF, 1), 0, N_SHOT - 1)
    position = jnp.arange(per_dev, dtype=jnp.int32)[None, None, :]
    cycled = (position - capacity + starting) % (N_SHOT - 1)
    others = cycled + (cycled >= hottest).astype(jnp.int32)
    owner_of = jnp.where(position < capacity, hottest, others)
    scores = jax.random.randint(jax.random.fold_in(seed_key, 4), (N_SHOT, N_OFF, per_dev), 0, 65536) * per_dev + position
    arrange = jnp.argsort(scores, axis=2, stable=True)
    owner_of = jnp.take_along_axis(owner_of, arrange, axis=2)
    slot_of = jax.random.randint(jax.random.fold_in(seed_key, 5), (N_SHOT, N_OFF, per_dev), 0, count_dev)
    identity = shuffle[owner_of * count_dev + slot_of]
    return (block_layout(identity), owners, places)


def bin_draw(seed_key):
    groups = jnp.arange(N_OFF, dtype=jnp.int32)[None, :, None]
    inside = jax.random.randint(seed_key, (N_SHOT, N_OFF, SHOT_DEV * TR_OFF), 0, OFFB_DEV)
    return block_layout(inside + groups * OFFB_DEV)


def draw_offset_bin(key, part):
    return bin_draw(jax.random.fold_in(key, 303))


def draw_rec_id(key, part):
    return trace_ids(jax.random.fold_in(key, 101), REC_DEV)[0]


def draw_rec_owner(key, part):
    return trace_ids(jax.random.fold_in(key, 101), REC_DEV)[1]


def draw_rec_slot(key, part):
    return trace_ids(jax.random.fold_in(key, 101), REC_DEV)[2]


def draw_cmp_id(key, part):
    return trace_ids(jax.random.fold_in(key, 202), CMP_DEV)[0]


def draw_cmp_owner(key, part):
    return trace_ids(jax.random.fold_in(key, 202), CMP_DEV)[1]


def draw_cmp_slot(key, part):
    return trace_ids(jax.random.fold_in(key, 202), CMP_DEV)[2]


def draw_traces(key, part):
    bins = bin_draw(jax.random.fold_in(key, 303))
    receivers = trace_ids(jax.random.fold_in(key, 101), REC_DEV)[0]
    midpoints = trace_ids(jax.random.fold_in(key, 202), CMP_DEV)[0]
    rec_gain = jax.random.uniform(jax.random.fold_in(key, 405), (NREC,), jnp.float32, -0.5, 0.5)
    cmp_gain = jax.random.uniform(jax.random.fold_in(key, 406), (NCMP,), jnp.float32, -0.4, 0.4)
    off_level = -1.0 * jnp.arange(NOFF, dtype=jnp.float32) / NOFF + jax.random.uniform(jax.random.fold_in(key, 407), (NOFF,), jnp.float32, -0.2, 0.2)
    shot_pos = jnp.arange(SHOTS, dtype=jnp.float32) / SHOTS
    jitter = jax.random.uniform(jax.random.fold_in(key, 408), (SHOTS,), jnp.float32, -0.3, 0.3)
    shot_level = 0.8 * shot_pos + jitter
    noise = jnp.clip(jax.random.normal(jax.random.fold_in(key, 409), (SHOTS, TR_SHOT, NT), jnp.float32), -6.0, 6.0)
    levels = shot_level[:, None] + off_level[bins] + rec_gain[receivers] + cmp_gain[midpoints]
    return jnp.clip(noise * jnp.exp(levels)[:, :, None], -60.0, 60.0).astype(jnp.bfloat16)


def setup_inputs(seed: int = 0) -> dict:
    keys = jax.random.split(jax.random.key(seed), 9)
    return {
        "traces": draw_traces(jax.random.fold_in(keys[8], 71), 0),
        "offset_bin": draw_offset_bin(jax.random.fold_in(keys[8], 71), 0),
        "rec_id": draw_rec_id(jax.random.fold_in(keys[8], 71), 0),
        "cmp_id": draw_cmp_id(jax.random.fold_in(keys[8], 71), 0),
        "rec_owner": draw_rec_owner(jax.random.fold_in(keys[8], 71), 0),
        "rec_slot": draw_rec_slot(jax.random.fold_in(keys[8], 71), 0),
        "cmp_owner": draw_cmp_owner(jax.random.fold_in(keys[8], 71), 0),
        "cmp_slot": draw_cmp_slot(jax.random.fold_in(keys[8], 71), 0),
    }


OMEGA = 0.35
FLOOR = 0.05

def spectral_table(samples, freqs):
    sample_idx = jnp.arange(samples, dtype=jnp.int32)
    freq_idx = jnp.arange(freqs, dtype=jnp.int32)
    phases = sample_idx[:, None] * freq_idx[None, :] % samples
    angles = phases.astype(jnp.float32) * (2.0 * math.pi / samples)
    tapers = 0.5 - 0.5 * jnp.cos((sample_idx.astype(jnp.float32) + 0.5) * (2.0 * math.pi / samples))
    weights = (tapers * math.sqrt(8.0 / (3.0 * samples)))[:, None]
    return jnp.concatenate([weights * jnp.cos(angles), -weights * jnp.sin(angles)], axis=1).astype(jnp.bfloat16)

def log_spectrum(shot_block, table, freqs):
    products = jnp.dot(shot_block, table, preferred_element_type=jnp.float32)
    real_part = products[:, :freqs]
    imag_part = products[:, freqs:]
    return jnp.log(real_part * real_part + imag_part * imag_part + FLOOR)

def reference(traces, offset_bin, rec_id, cmp_id, rec_owner, rec_slot, cmp_owner, cmp_slot):
    shots, tr_shot, samples = traces.shape
    table = spectral_table(samples, NF)
    logs = lax.map(lambda shot_block: log_spectrum(shot_block, table, NF), traces)
    bins = offset_bin.reshape(-1)
    receivers = rec_id.reshape(-1)
    midpoints = cmp_id.reshape(-1)
    unit = jnp.ones(bins.shape, jnp.float32)
    bin_count = jax.ops.segment_sum(unit, bins, NOFF)
    rec_count = jax.ops.segment_sum(unit, receivers, NREC)
    cmp_count = jax.ops.segment_sum(unit, midpoints, NCMP)
    source_term = jnp.zeros((shots, NF), jnp.float32)
    offset_term = jnp.zeros((NOFF, NF), jnp.float32)
    rec_term = jnp.zeros((NREC, NF), jnp.float32)
    cmp_term = jnp.zeros((NCMP, NF), jnp.float32)
    for sweep_no in range(SWEEPS):
        rec_trace = lax.optimization_barrier(rec_term.astype(jnp.bfloat16)).astype(jnp.float32)[receivers]
        cmp_trace = lax.optimization_barrier(cmp_term.astype(jnp.bfloat16)).astype(jnp.float32)[midpoints]
        per_shot = (logs - source_term[:, None, :]).reshape(shots * tr_shot, NF)
        residual = per_shot - offset_term[bins] - rec_trace - cmp_trace
        rounded = lax.optimization_barrier(residual.astype(jnp.bfloat16)).astype(jnp.float32)
        shot_sum = lax.optimization_barrier(jnp.sum(residual.reshape(shots, tr_shot, NF), axis=1))
        bin_sum = jax.ops.segment_sum(residual, bins, NOFF)
        rec_sum = jax.ops.segment_sum(rounded, receivers, NREC)
        cmp_sum = jax.ops.segment_sum(rounded, midpoints, NCMP)
        source_term = source_term + OMEGA * shot_sum / (tr_shot + 1.0)
        offset_term = offset_term + OMEGA * bin_sum / (bin_count[:, None] + 1.0)
        rec_term = rec_term + OMEGA * rec_sum / (rec_count[:, None] + 1.0)
        cmp_term = cmp_term + OMEGA * cmp_sum / (cmp_count[:, None] + 1.0)
    receiver_term = jnp.zeros_like(rec_term).at[rec_owner * REC_DEV + rec_slot].set(rec_term)
    midpoint_term = jnp.zeros_like(cmp_term).at[cmp_owner * CMP_DEV + cmp_slot].set(cmp_term)
    return (source_term, offset_term, receiver_term, midpoint_term)
```

```python
import math

import jax
import jax.numpy as jnp
import numpy as np
from jax import lax
from jax.experimental import pallas as pl
from jax.experimental.pallas import tpu as pltpu
from jax.sharding import PartitionSpec as P

NF = 640
OFFB_DEV = 8
SWEEPS = 2
LANES = 128
WIDE = 256
REM = 4
ITEMS = 16
ID_ROWS = 8

OMEGA = 0.35
FLOOR = 0.05
VMEM_BYTES = 60 * 1024 * 1024
HOT_BYTES = 40 * 1024 * 1024


def up(value, unit):
    return -(-value // unit) * unit


def dot_nt(a, b):
    return lax.dot_general(a, b, (((1,), (1,)), ((), ())), preferred_element_type=jnp.float32)


def dot_nn(a, b):
    return lax.dot_general(a, b, (((1,), (0,)), ((), ())), preferred_element_type=jnp.float32)


def group_count(n_dev):
    return 4 if n_dev % 4 == 0 else 1


def base_angles(samples, n_dev, held, main):
    groups = group_count(n_dev)
    dests = n_dev // groups
    rows = dests * (main + REM)
    row = np.arange(groups * rows)
    group, inside = row // rows, row % rows
    in_main = inside < dests * main
    rest = inside - dests * main
    dest = np.where(in_main, inside // max(main, 1), rest // REM)
    place = np.where(in_main, inside % max(main, 1), main + rest % REM)
    freq = ((group * dests + dest) * held + place)[:, None]
    step = 2.0 * math.pi / samples
    coarse = freq * (np.arange(samples // LANES)[None, :] * LANES) % samples * step
    fine = freq * np.arange(LANES)[None, :] % samples * step
    tapers = 0.5 - 0.5 * np.cos((np.arange(samples)[None, :] + 0.5) * step)
    weights = tapers * math.sqrt(8.0 / (3.0 * samples))
    tables = (np.cos(coarse), np.sin(coarse), np.cos(fine), np.sin(fine), weights)
    return tuple(table.astype(np.float32) for table in tables)


def remote(src, dst, send_sem, recv_sem, dest, n_off):
    return pltpu.make_async_remote_copy(
        src_ref=src,
        dst_ref=dst,
        send_sem=send_sem,
        recv_sem=recv_sem,
        device_id=(dest // n_off, dest % n_off),
        device_id_type=pl.DeviceIdType.MESH,
    )


def greet_all(me, n_dev, n_off):
    barrier = pltpu.get_barrier_semaphore()

    @pl.loop(1, n_dev)
    def _(step):
        dest = (me + step) % n_dev
        pl.semaphore_signal(
            barrier,
            inc=1,
            device_id=(dest // n_off, dest % n_off),
            device_id_type=pl.DeviceIdType.MESH,
        )

    return barrier


def lower_half(shape):
    return lax.broadcasted_iota(jnp.int32, shape, 0) >= REM


def fold(values):
    return values + pltpu.roll(values, REM, 0)


def terms_kernel(
    sizes,
    traces_ref,
    bin_ref,
    rec_ref,
    cmp_ref,
    ca_ref,
    sa_ref,
    cb_ref,
    sb_ref,
    w_ref,
    rec_owner_ref,
    rec_slot_ref,
    cmp_owner_ref,
    cmp_slot_ref,
    out_ref,
    stage,
    landed,
    table,
    raw,
    id_rows,
    ids,
    rec_tab,
    cmp_tab,
    iota_ref,
    hots,
    rec_acc,
    cmp_acc,
    rec_cnt,
    cmp_cnt,
    so_acc,
    rec_x,
    cmp_x,
    so_x,
    ret_stage,
    ret_landed,
    send_sems,
    recv_sems,
    line_send_sems,
    line_recv_sems,
    layer_send_sems,
    layer_recv_sems,
    ret_send_sems,
    ret_recv_sems,
    own_sems,
):
    n_shot, n_off, shot_dev, tr_off, rec_dev, cmp_dev, main = sizes
    n_dev = n_shot * n_off
    groups = group_count(n_dev)
    dests = n_dev // groups
    rows = dests * (main + REM)
    tr_dev, samples = traces_ref.shape
    half = tr_dev // 2
    rec_l = rec_cnt.shape[0]
    cmp_l = cmp_cnt.shape[0]
    rec_rows = rec_dev // n_off
    cmp_rows = cmp_dev // n_off
    keep_hots = hots.shape[0] == n_dev
    me = lax.axis_index("shot") * n_off + lax.axis_index("off")
    my_group = me // dests
    my_place = me % dests
    barrier = greet_all(me, n_dev, n_off)

    def block_copy(dest, slot):
        return remote(
            stage.at[dest], landed.at[slot], send_sems.at[dest], recv_sems.at[slot], dest, n_off
        )

    def line_copy(step, slot):
        block = ids.at[my_place, slot]
        dest = (my_group ^ step) * dests + my_place
        return remote(block, block, line_send_sems.at[step], line_recv_sems.at[step], dest, n_off)

    def layer_copy(place, slot):
        block = ids.at[slot]
        dest = my_group * dests + place
        return remote(block, block, layer_send_sems.at[place], layer_recv_sems.at[slot], dest, n_off)

    def return_copy(dest, slot):
        return remote(
            ret_stage.at[dest],
            ret_landed.at[slot],
            ret_send_sems.at[dest],
            ret_recv_sems.at[slot],
            dest,
            n_off,
        )

    def stage_logs(group):
        base = pl.multiple_of(group * rows, 8)
        cb = cb_ref[pl.ds(base, rows), :]
        sb = sb_ref[pl.ds(base, rows), :]
        ca_all = ca_ref[pl.ds(base, rows), :]
        sa_all = sa_ref[pl.ds(base, rows), :]
        for a in range(samples // LANES):
            cols = slice(a * LANES, (a + 1) * LANES)
            w = w_ref[:, cols]
            ca = ca_all[:, a : a + 1]
            sa = sa_all[:, a : a + 1]
            table[:rows, cols] = (w * (ca * cb - sa * sb)).astype(jnp.bfloat16)
            table[rows:, cols] = (-w * (sa * cb + ca * sb)).astype(jnp.bfloat16)
        products = dot_nt(table[...], traces_ref[...])
        real_part = products[:rows]
        imag_part = products[rows:]
        logs = jnp.log(real_part * real_part + imag_part * imag_part + FLOOR)
        first = group * dests
        if main:
            block = logs[: dests * main].reshape(dests, main, tr_dev).astype(jnp.bfloat16)
            stage[pl.ds(first, dests), :main, :] = block[:, :, :half]
            stage[pl.ds(first, dests), main : 2 * main, :] = block[:, :, half:]
        rest = logs[dests * main :]
        low = lower_half((2 * REM, half))
        for pair in range(dests // 2):
            both = rest[2 * REM * pair : 2 * REM * (pair + 1)]
            left, right = both[:, :half], both[:, half:]
            upper = jnp.where(low, pltpu.roll(right, REM, 0), left)
            lower = jnp.where(low, right, pltpu.roll(left, REM, 0))
            stage[first + 2 * pair, 2 * main :, :] = upper.astype(jnp.bfloat16)
            stage[first + 2 * pair + 1, 2 * main :, :] = lower.astype(jnp.bfloat16)

    def send_group(group, own):
        @pl.loop(1 if own else 0, dests)
        def _(step):
            block_copy(group * dests + (step + my_place) % dests, me).start()

    def one_hot_f32(index):
        row = lax.broadcasted_iota(jnp.int32, (WIDE, index.shape[1]), 0)
        return jnp.where(row == index, 1.0, 0.0).astype(jnp.bfloat16)

    def fill_table(tab, owner_ref, slot_ref, count_dev, levels):
        @pl.loop(0, levels)
        def _(level):
            span = pl.ds(pl.multiple_of(level * WIDE, WIDE), WIDE)
            position = (owner_ref[span] * count_dev + slot_ref[span]).reshape(1, WIDE)
            tab[pl.ds(level, 1), :] = (position // WIDE).astype(jnp.float32)
            tab[pl.ds(levels + level, 1), :] = (position % WIDE).astype(jnp.float32)

    def look_up(index, tab, levels):
        part = dot_nn(tab[...].astype(jnp.bfloat16), one_hot_f32(index % WIDE))
        level = lax.broadcasted_iota(jnp.int32, (levels, index.shape[1]), 0)
        mask = level == index // WIDE
        high = jnp.sum(jnp.where(mask, part[:levels], 0.0), axis=0, keepdims=True)
        low = jnp.sum(jnp.where(mask, part[levels:], 0.0), axis=0, keepdims=True)
        return low, high

    def own_ids():
        fill_table(rec_tab, rec_owner_ref, rec_slot_ref, rec_dev, rec_l)
        fill_table(cmp_tab, cmp_owner_ref, cmp_slot_ref, cmp_dev, cmp_l)
        for shot in range(shot_dev):
            cols = slice(shot * tr_off, (shot + 1) * tr_off)
            raw[0:1, cols] = rec_ref[shot : shot + 1, :]
            raw[1:2, cols] = cmp_ref[shot : shot + 1, :]
            raw[2:3, cols] = bin_ref[shot : shot + 1, :]
        id_rows[...] = jnp.zeros_like(id_rows)
        id_rows[0:1, :], id_rows[1:2, :] = look_up(raw[0:1, :], rec_tab, rec_l)
        id_rows[2:3, :], id_rows[3:4, :] = look_up(raw[1:2, :], cmp_tab, cmp_l)
        id_rows[4:5, :] = (raw[2:3, :] % OFFB_DEV).astype(jnp.float32)
        ids[my_place, my_group] = id_rows[...].astype(jnp.bfloat16)

    def send_line():
        for step in range(1, groups):
            line_copy(step, my_group).start()

    def send_layer():
        for step in range(1, groups):
            line_copy(step, my_group ^ step).wait_recv()

        @pl.loop(1, dests)
        def _(step):
            layer_copy((my_place + step) % dests, my_place).start()

    row_lane = lax.broadcasted_iota(jnp.int32, (WIDE, LANES), 0)
    iota_ref[...] = row_lane.astype(jnp.float32).astype(jnp.bfloat16)
    rec_acc[...] = jnp.zeros_like(rec_acc)
    cmp_acc[...] = jnp.zeros_like(cmp_acc)
    rec_cnt[...] = jnp.zeros_like(rec_cnt)
    cmp_cnt[...] = jnp.zeros_like(cmp_cnt)
    so_acc[...] = jnp.zeros_like(so_acc)

    turns = [3, 0, 2, 1] if groups == 4 else [0]
    for turn, mask in enumerate(turns):
        stage_logs(my_group ^ mask)
        if turn == 0:
            pl.semaphore_wait(barrier, n_dev - 1)
        send_group(my_group ^ mask, mask == 0)
        if turn == 0:
            own_ids()
            send_line()
        if turn == min(1, groups - 1):
            send_layer()
    own = pltpu.make_async_copy(stage.at[me], landed.at[me], own_sems.at[0])
    own.start()
    own.wait()

    @pl.loop(1, dests)
    def _(step):
        place = (my_place + dests - step) % dests
        layer_copy(place, place).wait_recv()

    chunks = main // 8
    low_full = lower_half((2 * REM, tr_dev))
    low_half = lower_half((2 * REM, half))
    local_shot = lax.broadcasted_iota(jnp.int32, (ITEMS, tr_dev), 1) // tr_off
    item_row = lax.broadcasted_iota(jnp.int32, (ITEMS, tr_dev), 0)
    shot_hot = item_row - OFFB_DEV == local_shot

    def make_hot(index):
        column = index.astype(jnp.bfloat16)
        one = jnp.ones((), jnp.bfloat16)
        zero = jnp.zeros((), jnp.bfloat16)
        parts = []
        for a in range(tr_dev // LANES):
            cols = slice(a * LANES, (a + 1) * LANES)
            parts.append(jnp.where(iota_ref[...] == column[:, cols], one, zero))
        return jnp.concatenate(parts, axis=1)

    def level_masks(index, levels):
        level = jnp.broadcast_to(index, (8, tr_dev))
        odd = jnp.where(low_full, level - 1.0, level)
        return (
            lambda l: level == float(l),
            lambda pair: odd == float(2 * pair),
        )

    def spread(mains, rest, index, levels):
        is_level, is_pair = level_masks(index, levels)
        parts = []
        if chunks:
            for l in range(levels):
                mask = is_level(l)
                parts += [jnp.where(mask, part, 0.0) for part in mains]
        for pair in range(levels // 2):
            parts.append(jnp.where(is_pair(pair), rest, 0.0))
        return parts

    def gather(part, index, levels):
        is_level, is_pair = level_masks(index, levels)
        mains = [0.0] * chunks
        if chunks:
            for l in range(levels):
                mask = is_level(l)
                for c in range(chunks):
                    start = l * main + 8 * c
                    mains[c] = mains[c] + jnp.where(mask, part[start : start + 8], 0.0)
        rest = 0.0
        for pair in range(levels // 2):
            start = levels * main + 8 * pair
            rest = rest + jnp.where(is_pair(pair), part[start : start + 8], 0.0)
        return mains, fold(rest)

    def add_source(src, first):
        block = landed[src].astype(jnp.float32)
        rest = block[2 * main :]
        turned = pltpu.roll(rest, REM, 0)
        rest = jnp.concatenate(
            [jnp.where(low_half, turned, rest), jnp.where(low_half, rest, turned)], axis=1
        )
        mains = [
            jnp.concatenate(
                [block[8 * c : 8 * c + 8], block[main + 8 * c : main + 8 * c + 8]], axis=1
            )
            for c in range(chunks)
        ]
        keys = ids[src % dests, src // dests].astype(jnp.float32)
        rec_low, rec_high, cmp_low, cmp_high, bins = (keys[k : k + 1] for k in range(5))
        so_hot = (item_row.astype(jnp.float32) == bins) | shot_hot
        so_hot = jnp.where(so_hot, 1.0, 0.0).astype(jnp.bfloat16)
        if first or not keep_hots:
            rec_hot = make_hot(rec_low)
            cmp_hot = make_hot(cmp_low)
            if keep_hots:
                hots[src, 0] = rec_hot
                hots[src, 1] = cmp_hot
        else:
            rec_hot = hots[src, 0]
            cmp_hot = hots[src, 1]
        if not first:
            so_part = dot_nn(so_x[src][:, :ITEMS], so_hot)
            held = main + 2 * REM
            so_part = so_part[:held] + so_part[held:]
            rec_mains, rec_rest = gather(dot_nn(rec_x[...], rec_hot), rec_high, rec_l)
            cmp_mains, cmp_rest = gather(dot_nn(cmp_x[...], cmp_hot), cmp_high, cmp_l)
            for c in range(chunks):
                mains[c] = mains[c] - so_part[8 * c : 8 * c + 8] - rec_mains[c] - cmp_mains[c]
            rest = rest - so_part[main:] - rec_rest - cmp_rest
        rec_parts = spread(mains, rest, rec_high, rec_l)
        cmp_parts = spread(mains, rest, cmp_high, cmp_l)
        so_parts = mains + [rest]
        if first:
            for parts, index, levels in ((rec_parts, rec_high, rec_l), (cmp_parts, cmp_high, cmp_l)):
                level = lax.broadcasted_iota(jnp.int32, (levels, tr_dev), 0)
                parts.append(jnp.where(level.astype(jnp.float32) == index, 1.0, 0.0))
            so_parts = so_parts + [jnp.ones((8, tr_dev), jnp.float32)]
        join = lambda parts: jnp.concatenate(parts, axis=0).astype(jnp.bfloat16)
        rec_sum = dot_nt(join(rec_parts), rec_hot)
        cmp_sum = dot_nt(join(cmp_parts), cmp_hot)
        so_sum = dot_nt(join(so_parts), so_hot)
        rec_acc[...] += rec_sum[: rec_acc.shape[0]]
        cmp_acc[...] += cmp_sum[: cmp_acc.shape[0]]
        if first:
            rec_cnt[...] += rec_sum[rec_acc.shape[0] :]
            cmp_cnt[...] += cmp_sum[cmp_acc.shape[0] :]
            so_acc[src, :, 0:ITEMS] = so_sum
        else:
            so_acc[src, 0 : main + 2 * REM, 0:ITEMS] += so_sum

    order = [0, 1, 3, 2] if groups == 4 else [0]

    def first_pass(mask):
        @pl.loop(0, dests)
        def _(step):
            src = (my_group ^ mask) * dests + (my_place + dests - step) % dests
            if mask == 0:

                @pl.when(step > 0)
                def _():
                    block_copy(src, src).wait_recv()

            else:
                block_copy(src, src).wait_recv()
            add_source(src, True)

    for mask in order:
        first_pass(mask)

    held = main + 2 * REM

    def so_terms():
        sums = so_acc[...].reshape(n_shot, n_off, so_acc.shape[1], LANES)
        bins = jnp.sum(sums, axis=0)
        shots = jnp.sum(sums, axis=1)
        lane = lax.broadcasted_iota(jnp.int32, sums.shape, 3)
        both = jnp.where(lane < OFFB_DEV, bins[None], shots[:, None])
        both = both.reshape(so_acc.shape)
        return OMEGA * both[:, :held] / (both[:, held : held + 1] + 1.0)

    def scaled(acc, cnt, cols):
        levels = cnt.shape[0]
        width = cols.stop - cols.start
        low = lower_half((2 * REM, width))

        def main_part(l):
            return acc[l * main : (l + 1) * main, cols] * cnt[l : l + 1, cols]

        def pair_part(pair):
            scale = jnp.where(low, cnt[2 * pair + 1 : 2 * pair + 2, cols], cnt[2 * pair : 2 * pair + 1, cols])
            start = levels * main + 2 * REM * pair
            return acc[start : start + 2 * REM, cols] * scale

        return main_part, pair_part

    rec_cnt[...] = OMEGA / (rec_cnt[...] + 1.0)
    cmp_cnt[...] = OMEGA / (cmp_cnt[...] + 1.0)

    def refresh(x, acc, cnt):
        levels = cnt.shape[0]
        main_part, pair_part = scaled(acc, cnt, slice(0, WIDE))
        parts = [main_part(l) for l in range(levels)] if main else []
        parts += [pair_part(pair) for pair in range(levels // 2)]
        x[...] = jnp.concatenate(parts, axis=0).astype(jnp.bfloat16)

    for _ in range(SWEEPS - 1):
        refresh(rec_x, rec_acc, rec_cnt)
        refresh(cmp_x, cmp_acc, cmp_cnt)
        so = so_terms()
        so_high = so.astype(jnp.bfloat16).astype(jnp.float32)
        so_x[...] = jnp.concatenate([so_high, so - so_high], axis=1).astype(jnp.bfloat16)

        @pl.loop(0, n_dev)
        def _(src):
            add_source(src, False)

    so = so_terms()
    lane8 = lax.broadcasted_iota(jnp.int32, (8, LANES), 1)
    low8 = lower_half((8, LANES))

    def at_zero(values, offset):
        return values if offset == 0 else pltpu.roll(values, LANES - offset, 1)

    for dest in range(n_dev):
        cmp_level, cmp_at = divmod(dest * cmp_rows, WIDE)
        rec_level, rec_at = divmod(dest * rec_rows, WIDE)
        cmp_from, cmp_off = divmod(cmp_at, LANES)
        rec_from, rec_off = divmod(rec_at, LANES)
        cmp_main, cmp_pair = scaled(cmp_acc, cmp_cnt, slice(cmp_from * LANES, (cmp_from + 1) * LANES))
        rec_main, rec_pair = scaled(rec_acc, rec_cnt, slice(rec_from * LANES, (rec_from + 1) * LANES))
        extra = pltpu.roll(so[dest], rec_rows, 1)
        if main:
            ret_stage[dest, :main, :] = at_zero(cmp_main(cmp_level), cmp_off).astype(jnp.bfloat16)
            values = at_zero(rec_main(rec_level), rec_off)
            lane = lax.broadcasted_iota(jnp.int32, values.shape, 1)
            values = jnp.where(lane < rec_rows, values, extra[:main])
            ret_stage[dest, main + 8 :, :] = values.astype(jnp.bfloat16)
        cmp_rest = at_zero(cmp_pair(cmp_level // 2), cmp_off)
        if cmp_level % 2 == 1:
            cmp_rest = pltpu.roll(cmp_rest, REM, 0)
        rec_rest = at_zero(rec_pair(rec_level // 2), rec_off)
        if rec_level % 2 == 0:
            rec_rest = pltpu.roll(rec_rest, REM, 0)
        rec_rest = jnp.where(lane8 < rec_rows, rec_rest, extra[main:])
        ret_stage[dest, main : main + 8, :] = jnp.where(low8, rec_rest, cmp_rest).astype(jnp.bfloat16)

    own = pltpu.make_async_copy(ret_stage.at[me], ret_landed.at[me], own_sems.at[1])
    own.start()
    for mask in (3, 2, 1, 0) if groups == 4 else (0,):

        @pl.loop(1 if mask == 0 else 0, dests)
        def _(step):
            return_copy((my_group ^ mask) * dests + (step + my_place) % dests, me).start()

    @pl.loop(1, n_dev)
    def _(step):
        dest = (me + step) % n_dev
        block_copy(dest, me).wait_send()

    for step in range(1, groups):
        line_copy(step, my_group).wait_send()

    @pl.loop(1, dests)
    def _(step):
        layer_copy((my_place + step) % dests, my_place).wait_send()

    own.wait()

    @pl.loop(1, n_dev)
    def _(step):
        dest = (me + step) % n_dev
        return_copy(dest, me).wait_send()
        return_copy(dest, dest).wait_recv()

    out_ref[...] = ret_landed[...]


def run_terms(traces, ids, owners, sizes, held):
    n_shot, n_off, shot_dev, tr_off, rec_dev, cmp_dev, main = sizes
    n_dev = n_shot * n_off
    tr_dev, samples = traces.shape
    groups = group_count(n_dev)
    dests = n_dev // groups
    rows = dests * (main + REM)
    rec_l = owners[0].shape[0] // WIDE
    cmp_l = owners[2].shape[0] // WIDE
    tables = base_angles(samples, n_dev, held, main)
    vmem = pl.BlockSpec(memory_space=pltpu.VMEM)
    block = (n_dev, 2 * main + 2 * REM, tr_dev // 2)
    ret_block = (n_dev, 2 * main + 8, LANES)
    hot_bytes = n_dev * 2 * WIDE * tr_dev * 2
    kept = n_dev if hot_bytes <= HOT_BYTES else 1
    count = main + REM
    return pl.pallas_call(
        lambda *refs: terms_kernel(sizes, *refs),
        out_shape=jax.ShapeDtypeStruct(ret_block, jnp.bfloat16),
        in_specs=[vmem] * 13,
        out_specs=vmem,
        scratch_shapes=[
            pltpu.VMEM(block, jnp.bfloat16),
            pltpu.VMEM(block, jnp.bfloat16),
            pltpu.VMEM((2 * rows, samples), jnp.bfloat16),
            pltpu.VMEM((8, tr_dev), jnp.int32),
            pltpu.VMEM((ID_ROWS, tr_dev), jnp.float32),
            pltpu.VMEM((dests, groups, ID_ROWS, tr_dev), jnp.bfloat16),
            pltpu.VMEM((2 * rec_l, WIDE), jnp.float32),
            pltpu.VMEM((2 * cmp_l, WIDE), jnp.float32),
            pltpu.VMEM((WIDE, LANES), jnp.bfloat16),
            pltpu.VMEM((kept, 2, WIDE, tr_dev), jnp.bfloat16),
            pltpu.VMEM((rec_l * count, WIDE), jnp.float32),
            pltpu.VMEM((cmp_l * count, WIDE), jnp.float32),
            pltpu.VMEM((rec_l, WIDE), jnp.float32),
            pltpu.VMEM((cmp_l, WIDE), jnp.float32),
            pltpu.VMEM((n_dev, main + 2 * REM + 8, LANES), jnp.float32),
            pltpu.VMEM((rec_l * count, WIDE), jnp.bfloat16),
            pltpu.VMEM((cmp_l * count, WIDE), jnp.bfloat16),
            pltpu.VMEM((n_dev, 2 * (main + 2 * REM), LANES), jnp.bfloat16),
            pltpu.VMEM(ret_block, jnp.bfloat16),
            pltpu.VMEM(ret_block, jnp.bfloat16),
            pltpu.SemaphoreType.DMA((n_dev,)),
            pltpu.SemaphoreType.DMA((n_dev,)),
            pltpu.SemaphoreType.DMA((groups,)),
            pltpu.SemaphoreType.DMA((groups,)),
            pltpu.SemaphoreType.DMA((dests,)),
            pltpu.SemaphoreType.DMA((dests,)),
            pltpu.SemaphoreType.DMA((n_dev,)),
            pltpu.SemaphoreType.DMA((n_dev,)),
            pltpu.SemaphoreType.DMA((2,)),
        ],
        compiler_params=pltpu.CompilerParams(
            vmem_limit_bytes=VMEM_BYTES, collective_id=0, has_side_effects=True
        ),
        name="terms",
    )(traces, *ids, *tables, *owners)


def output_kernel(sizes, held, blocks_ref, source_ref, offset_ref, rec_ref, cmp_ref, joined):
    shot_dev, rec_rows, cmp_rows, main = sizes
    n_dev = blocks_ref.shape[0]
    for src in range(n_dev):
        rows = min(held, NF - src * held)
        if rows > 0:
            block = blocks_ref[src].astype(jnp.float32)
            start = src * held
            joined[start : start + rows, :LANES] = block[:rows]
            first = min(main, rows)
            if first:
                joined[start : start + first, LANES:] = block[main + 8 : main + 8 + first]
            if rows > main:
                joined[start + main : start + rows, LANES:] = block[main + REM : REM + rows]
    turned = joined[...].T
    cmp_ref[...] = turned[:cmp_rows]
    rec_ref[...] = turned[LANES : LANES + rec_rows]
    base = LANES + rec_rows
    offset_ref[...] = turned[base : base + OFFB_DEV]
    source_ref[...] = turned[base + OFFB_DEV : base + OFFB_DEV + shot_dev]


def write_outputs(blocks, sizes, held):
    shot_dev, rec_rows, cmp_rows, main = sizes
    vmem = pl.BlockSpec(memory_space=pltpu.VMEM)
    shape = lambda rows: jax.ShapeDtypeStruct((rows, NF), jnp.float32)
    return pl.pallas_call(
        lambda *refs: output_kernel(sizes, held, *refs),
        out_shape=(shape(shot_dev), shape(OFFB_DEV), shape(rec_rows), shape(cmp_rows)),
        in_specs=[vmem],
        out_specs=(vmem,) * 4,
        scratch_shapes=[pltpu.VMEM((NF, 2 * LANES), jnp.float32)],
        compiler_params=pltpu.CompilerParams(vmem_limit_bytes=VMEM_BYTES),
        name="outputs",
    )(blocks)


def shards(traces, offset_bin, rec_id, cmp_id, rec_owner, rec_slot, cmp_owner, cmp_slot):
    shot_dev, tr_off, samples = traces.shape
    n_shot = lax.axis_size("shot")
    n_off = lax.axis_size("off")
    n_dev = n_shot * n_off
    tr_dev = shot_dev * tr_off
    rec_dev = rec_owner.shape[0] // n_shot
    cmp_dev = cmp_owner.shape[0] // n_shot
    held = up(NF, n_dev) // n_dev
    main = up(max(held - REM, 0), 8)
    blocks = run_terms(
        traces.reshape(tr_dev, samples),
        (offset_bin, rec_id, cmp_id),
        (rec_owner, rec_slot, cmp_owner, cmp_slot),
        (n_shot, n_off, shot_dev, tr_off, rec_dev, cmp_dev, main),
        held,
    )
    sizes = (shot_dev, rec_dev // n_off, cmp_dev // n_off, main)
    return write_outputs(blocks, sizes, held)


def solution(mesh):
    return jax.shard_map(
        shards,
        mesh=mesh,
        in_specs=(
            P("shot", "off", None),
            P("shot", "off"),
            P("shot", "off"),
            P("shot", "off"),
            P(),
            P(),
            P(),
            P(),
        ),
        out_specs=(
            P("shot", None),
            P("off", None),
            P(("shot", "off"), None),
            P(("shot", "off"), None),
        ),
        check_vma=False,
    )
```

```python
import math

import jax
import jax.numpy as jnp
import numpy as np
from jax import lax
from jax.experimental import pallas as pl
from jax.experimental.pallas import tpu as pltpu
from jax.sharding import PartitionSpec as P

NF = 640
OFFB_DEV = 8
SWEEPS = 2
LANES = 128
WIDE = 256
REM = 4
ITEMS = 16
ID_ROWS = 8

OMEGA = 0.35
FLOOR = 0.05
VMEM_BYTES = 60 * 1024 * 1024
HOT_BYTES = 40 * 1024 * 1024


def up(value, unit):
    return -(-value // unit) * unit


def dot_nt(a, b):
    return lax.dot_general(a, b, (((1,), (1,)), ((), ())), preferred_element_type=jnp.float32)


def dot_nn(a, b):
    return lax.dot_general(a, b, (((1,), (0,)), ((), ())), preferred_element_type=jnp.float32)


def group_count(n_dev):
    return 4 if n_dev % 4 == 0 else 1


def base_angles(samples, n_dev, held, main):
    groups = group_count(n_dev)
    dests = n_dev // groups
    rows = dests * (main + REM)
    row = np.arange(groups * rows)
    group, inside = row // rows, row % rows
    in_main = inside < dests * main
    rest = inside - dests * main
    dest = np.where(in_main, inside // max(main, 1), rest // REM)
    place = np.where(in_main, inside % max(main, 1), main + rest % REM)
    freq = ((group * dests + dest) * held + place)[:, None]
    step = 2.0 * math.pi / samples
    coarse = freq * (np.arange(samples // LANES)[None, :] * LANES) % samples * step
    fine = freq * np.arange(LANES)[None, :] % samples * step
    tapers = 0.5 - 0.5 * np.cos((np.arange(samples)[None, :] + 0.5) * step)
    weights = tapers * math.sqrt(8.0 / (3.0 * samples))
    tables = (np.cos(coarse), np.sin(coarse), np.cos(fine), np.sin(fine), weights)
    return tuple(table.astype(np.float32) for table in tables)


def remote(src, dst, send_sem, recv_sem, dest, n_off):
    return pltpu.make_async_remote_copy(
        src_ref=src,
        dst_ref=dst,
        send_sem=send_sem,
        recv_sem=recv_sem,
        device_id=(dest // n_off, dest % n_off),
        device_id_type=pl.DeviceIdType.MESH,
    )


def greet_all(me, n_dev, n_off):
    barrier = pltpu.get_barrier_semaphore()

    @pl.loop(1, n_dev)
    def _(step):
        dest = (me + step) % n_dev
        pl.semaphore_signal(
            barrier,
            inc=1,
            device_id=(dest // n_off, dest % n_off),
            device_id_type=pl.DeviceIdType.MESH,
        )

    return barrier


def lower_half(shape):
    return lax.broadcasted_iota(jnp.int32, shape, 0) >= REM


def fold(values):
    return values + pltpu.roll(values, REM, 0)


def plan_of(groups, dests):
    half = dests // 2
    if groups != 4:
        return [
            ("logs", 0, 0, 0),
            ("layer", 0, 0, 0),
            ("send", 0, 0, dests),
            ("settle", 0, 0, 0),
            ("add", 0, 0, dests),
        ]
    return [
        ("logs", 3, 0, 0),
        ("send", 3, 0, half),
        ("layer", 0, 0, 0),
        ("logs", 2, 0, 0),
        ("send", 3, half, dests),
        ("send", 2, 0, half),
        ("logs", 0, 0, 0),
        ("send", 0, 0, dests),
        ("logs", 1, 0, 0),
        ("settle", 0, 0, 0),
        ("send", 2, half, dests),
        ("add", 0, 0, dests),
        ("send", 1, 0, dests),
        ("add", 3, 0, dests),
        ("add", 1, 0, dests),
        ("add", 2, 0, dests),
    ]


def terms_kernel(
    sizes,
    traces_ref,
    bin_ref,
    rec_ref,
    cmp_ref,
    ca_ref,
    sa_ref,
    cb_ref,
    sb_ref,
    w_ref,
    rec_owner_ref,
    rec_slot_ref,
    cmp_owner_ref,
    cmp_slot_ref,
    out_ref,
    stage,
    landed,
    table,
    raw,
    id_rows,
    ids,
    rec_tab,
    cmp_tab,
    iota_ref,
    hots,
    rec_acc,
    cmp_acc,
    rec_cnt,
    cmp_cnt,
    so_acc,
    rec_x,
    cmp_x,
    so_x,
    ret_stage,
    ret_landed,
    send_sems,
    recv_sems,
    line_send_sems,
    line_recv_sems,
    layer_send_sems,
    layer_recv_sems,
    ret_send_sems,
    ret_recv_sems,
    own_sems,
):
    n_shot, n_off, shot_dev, tr_off, rec_dev, cmp_dev, main = sizes
    n_dev = n_shot * n_off
    groups = group_count(n_dev)
    dests = n_dev // groups
    rows = dests * (main + REM)
    tr_dev, samples = traces_ref.shape
    half = tr_dev // 2
    rec_l = rec_cnt.shape[0]
    cmp_l = cmp_cnt.shape[0]
    rec_rows = rec_dev // n_off
    cmp_rows = cmp_dev // n_off
    keep_hots = hots.shape[0] == n_dev
    me = lax.axis_index("shot") * n_off + lax.axis_index("off")
    my_group = me // dests
    my_place = me % dests
    barrier = greet_all(me, n_dev, n_off)

    def block_copy(dest, slot):
        return remote(
            stage.at[dest], landed.at[slot], send_sems.at[dest], recv_sems.at[slot], dest, n_off
        )

    def line_copy(step, slot):
        block = ids.at[my_place, slot]
        dest = (my_group ^ step) * dests + my_place
        return remote(block, block, line_send_sems.at[step], line_recv_sems.at[step], dest, n_off)

    def layer_copy(place, slot):
        block = ids.at[slot]
        dest = my_group * dests + place
        return remote(block, block, layer_send_sems.at[place], layer_recv_sems.at[slot], dest, n_off)

    def return_copy(dest, slot):
        return remote(
            ret_stage.at[dest],
            ret_landed.at[slot],
            ret_send_sems.at[dest],
            ret_recv_sems.at[slot],
            dest,
            n_off,
        )

    def stage_logs(group):
        base = pl.multiple_of(group * rows, 8)
        cb = cb_ref[pl.ds(base, rows), :]
        sb = sb_ref[pl.ds(base, rows), :]
        ca_all = ca_ref[pl.ds(base, rows), :]
        sa_all = sa_ref[pl.ds(base, rows), :]
        for a in range(samples // LANES):
            cols = slice(a * LANES, (a + 1) * LANES)
            w = w_ref[:, cols]
            ca = ca_all[:, a : a + 1]
            sa = sa_all[:, a : a + 1]
            table[:rows, cols] = (w * (ca * cb - sa * sb)).astype(jnp.bfloat16)
            table[rows:, cols] = (-w * (sa * cb + ca * sb)).astype(jnp.bfloat16)
        products = dot_nt(table[...], traces_ref[...])
        real_part = products[:rows]
        imag_part = products[rows:]
        logs = jnp.log(real_part * real_part + imag_part * imag_part + FLOOR)
        first = group * dests
        if main:
            block = logs[: dests * main].reshape(dests, main, tr_dev).astype(jnp.bfloat16)
            stage[pl.ds(first, dests), :main, :] = block[:, :, :half]
            stage[pl.ds(first, dests), main : 2 * main, :] = block[:, :, half:]
        rest = logs[dests * main :]
        low = lower_half((2 * REM, half))
        for pair in range(dests // 2):
            both = rest[2 * REM * pair : 2 * REM * (pair + 1)]
            left, right = both[:, :half], both[:, half:]
            upper = jnp.where(low, pltpu.roll(right, REM, 0), left)
            lower = jnp.where(low, right, pltpu.roll(left, REM, 0))
            stage[first + 2 * pair, 2 * main :, :] = upper.astype(jnp.bfloat16)
            stage[first + 2 * pair + 1, 2 * main :, :] = lower.astype(jnp.bfloat16)

    def one_hot_f32(index):
        row = lax.broadcasted_iota(jnp.int32, (WIDE, index.shape[1]), 0)
        return jnp.where(row == index, 1.0, 0.0).astype(jnp.bfloat16)

    def fill_table(tab, owner_ref, slot_ref, count_dev, levels):
        @pl.loop(0, levels)
        def _(level):
            span = pl.ds(pl.multiple_of(level * WIDE, WIDE), WIDE)
            position = (owner_ref[span] * count_dev + slot_ref[span]).reshape(1, WIDE)
            tab[pl.ds(level, 1), :] = (position // WIDE).astype(jnp.float32)
            tab[pl.ds(levels + level, 1), :] = (position % WIDE).astype(jnp.float32)

    def look_up(index, tab, levels):
        part = dot_nn(tab[...].astype(jnp.bfloat16), one_hot_f32(index % WIDE))
        level = lax.broadcasted_iota(jnp.int32, (levels, index.shape[1]), 0)
        mask = level == index // WIDE
        high = jnp.sum(jnp.where(mask, part[:levels], 0.0), axis=0, keepdims=True)
        low = jnp.sum(jnp.where(mask, part[levels:], 0.0), axis=0, keepdims=True)
        return low, high

    def own_ids():
        fill_table(rec_tab, rec_owner_ref, rec_slot_ref, rec_dev, rec_l)
        fill_table(cmp_tab, cmp_owner_ref, cmp_slot_ref, cmp_dev, cmp_l)
        for shot in range(shot_dev):
            cols = slice(shot * tr_off, (shot + 1) * tr_off)
            raw[0:1, cols] = rec_ref[shot : shot + 1, :]
            raw[1:2, cols] = cmp_ref[shot : shot + 1, :]
            raw[2:3, cols] = bin_ref[shot : shot + 1, :]
        id_rows[...] = jnp.zeros_like(id_rows)
        id_rows[0:1, :], id_rows[1:2, :] = look_up(raw[0:1, :], rec_tab, rec_l)
        id_rows[2:3, :], id_rows[3:4, :] = look_up(raw[1:2, :], cmp_tab, cmp_l)
        id_rows[4:5, :] = (raw[2:3, :] % OFFB_DEV).astype(jnp.float32)
        ids[my_place, my_group] = id_rows[...].astype(jnp.bfloat16)

    def send_line():
        for step in range(1, groups):
            line_copy(step, my_group).start()

    def send_layer():
        for step in range(1, groups):
            line_copy(step, my_group ^ step).wait_recv()

        @pl.loop(1, dests)
        def _(step):
            layer_copy((my_place + step) % dests, my_place).start()

    row_lane = lax.broadcasted_iota(jnp.int32, (WIDE, LANES), 0)
    iota_ref[...] = row_lane.astype(jnp.float32).astype(jnp.bfloat16)
    rec_acc[...] = jnp.zeros_like(rec_acc)
    cmp_acc[...] = jnp.zeros_like(cmp_acc)
    rec_cnt[...] = jnp.zeros_like(rec_cnt)
    cmp_cnt[...] = jnp.zeros_like(cmp_cnt)
    so_acc[...] = jnp.zeros_like(so_acc)

    own_ids()
    pl.semaphore_wait(barrier, n_dev - 1)
    send_line()
    chunks = main // 8
    low_full = lower_half((2 * REM, tr_dev))
    low_half = lower_half((2 * REM, half))
    local_shot = lax.broadcasted_iota(jnp.int32, (ITEMS, tr_dev), 1) // tr_off
    item_row = lax.broadcasted_iota(jnp.int32, (ITEMS, tr_dev), 0)
    shot_hot = item_row - OFFB_DEV == local_shot

    row_base = lax.broadcasted_iota(jnp.int32, (16, LANES), 0).astype(jnp.float32)
    row_base = row_base.astype(jnp.bfloat16)

    def make_hot(index):
        column = jnp.broadcast_to(index, (16, tr_dev)).astype(jnp.bfloat16)
        one = jnp.ones((), jnp.bfloat16)
        zero = jnp.zeros((), jnp.bfloat16)
        parts = []
        for i in range(WIDE // 16):
            row = row_base + jnp.full((), 16 * i, jnp.bfloat16)
            pieces = []
            for a in range(tr_dev // LANES):
                piece = column[:, a * LANES : (a + 1) * LANES]
                pieces.append(jnp.where(row == piece, one, zero))
            parts.append(jnp.concatenate(pieces, axis=1))
        return jnp.concatenate(parts, axis=0)

    def level_masks(index, levels):
        level = jnp.broadcast_to(index, (8, tr_dev))
        odd = jnp.where(low_full, level - 1.0, level)
        return (
            lambda l: level == float(l),
            lambda pair: odd == float(2 * pair),
        )

    def spread(mains, rest, index, levels):
        is_level, is_pair = level_masks(index, levels)
        parts = []
        if chunks:
            for l in range(levels):
                mask = is_level(l)
                parts += [jnp.where(mask, part, 0.0) for part in mains]
        for pair in range(levels // 2):
            parts.append(jnp.where(is_pair(pair), rest, 0.0))
        return parts

    def gather(part, index, levels):
        is_level, is_pair = level_masks(index, levels)
        mains = [0.0] * chunks
        if chunks:
            for l in range(levels):
                mask = is_level(l)
                for c in range(chunks):
                    start = l * main + 8 * c
                    mains[c] = mains[c] + jnp.where(mask, part[start : start + 8], 0.0)
        rest = 0.0
        for pair in range(levels // 2):
            start = levels * main + 8 * pair
            rest = rest + jnp.where(is_pair(pair), part[start : start + 8], 0.0)
        return mains, fold(rest)

    def add_source(src, first):
        block = landed[src].astype(jnp.float32)
        rest = block[2 * main :]
        turned = pltpu.roll(rest, REM, 0)
        rest = jnp.concatenate(
            [jnp.where(low_half, turned, rest), jnp.where(low_half, rest, turned)], axis=1
        )
        mains = [
            jnp.concatenate(
                [block[8 * c : 8 * c + 8], block[main + 8 * c : main + 8 * c + 8]], axis=1
            )
            for c in range(chunks)
        ]
        keys = ids[src % dests, src // dests].astype(jnp.float32)
        rec_low, rec_high, cmp_low, cmp_high, bins = (keys[k : k + 1] for k in range(5))
        so_hot = (item_row.astype(jnp.float32) == bins) | shot_hot
        so_hot = jnp.where(so_hot, 1.0, 0.0).astype(jnp.bfloat16)
        if first or not keep_hots:
            rec_hot = make_hot(rec_low)
            cmp_hot = make_hot(cmp_low)
            if keep_hots:
                hots[src, 0] = rec_hot
                hots[src, 1] = cmp_hot
        else:
            rec_hot = hots[src, 0]
            cmp_hot = hots[src, 1]
        if not first:
            so_part = dot_nn(so_x[src][:, :ITEMS], so_hot)
            held = main + 2 * REM
            so_part = so_part[:held] + so_part[held:]
            rec_mains, rec_rest = gather(dot_nn(rec_x[...], rec_hot), rec_high, rec_l)
            cmp_mains, cmp_rest = gather(dot_nn(cmp_x[...], cmp_hot), cmp_high, cmp_l)
            for c in range(chunks):
                mains[c] = mains[c] - so_part[8 * c : 8 * c + 8] - rec_mains[c] - cmp_mains[c]
            rest = rest - so_part[main:] - rec_rest - cmp_rest
        rec_parts = spread(mains, rest, rec_high, rec_l)
        cmp_parts = spread(mains, rest, cmp_high, cmp_l)
        so_parts = mains + [rest]
        if first:
            for parts, index, levels in ((rec_parts, rec_high, rec_l), (cmp_parts, cmp_high, cmp_l)):
                level = lax.broadcasted_iota(jnp.int32, (levels, tr_dev), 0)
                parts.append(jnp.where(level.astype(jnp.float32) == index, 1.0, 0.0))
            so_parts = so_parts + [jnp.ones((8, tr_dev), jnp.float32)]
        join = lambda parts: jnp.concatenate(parts, axis=0).astype(jnp.bfloat16)
        rec_sum = dot_nt(join(rec_parts), rec_hot)
        cmp_sum = dot_nt(join(cmp_parts), cmp_hot)
        so_sum = dot_nt(join(so_parts), so_hot)
        rec_acc[...] += rec_sum[: rec_acc.shape[0]]
        cmp_acc[...] += cmp_sum[: cmp_acc.shape[0]]
        if first:
            rec_cnt[...] += rec_sum[rec_acc.shape[0] :]
            cmp_cnt[...] += cmp_sum[cmp_acc.shape[0] :]
            so_acc[src, :, 0:ITEMS] = so_sum
        else:
            so_acc[src, 0 : main + 2 * REM, 0:ITEMS] += so_sum

    def send_part(mask, low, high):
        @pl.loop(max(low, 1) if mask == 0 else low, high)
        def _(step):
            block_copy((my_group ^ mask) * dests + (step + my_place) % dests, me).start()

    def drain_part(mask, low, high):
        @pl.loop(max(low, 1) if mask == 0 else low, high)
        def _(step):
            block_copy((my_group ^ mask) * dests + (step + my_place) % dests, me).wait_send()

    def add_part(mask, low, high):
        @pl.loop(low, high)
        def _(step):
            src = (my_group ^ mask) * dests + (my_place + dests - step) % dests
            if mask == 0 and low == 0:

                @pl.when(step > 0)
                def _():
                    block_copy(src, src).wait_recv()

            else:
                block_copy(src, src).wait_recv()
            add_source(src, True)

    def settle_own():
        own = pltpu.make_async_copy(stage.at[me], landed.at[me], own_sems.at[0])
        own.start()
        own.wait()

        @pl.loop(1, dests)
        def _(step):
            place = (my_place + dests - step) % dests
            layer_copy(place, place).wait_recv()

    plan = plan_of(groups, dests)
    for name, mask, low, high in plan:
        if name == "logs":
            stage_logs(my_group ^ mask)
        elif name == "layer":
            send_layer()
        elif name == "send":
            send_part(mask, low, high)
        elif name == "drain":
            drain_part(mask, low, high)
        elif name == "settle":
            settle_own()
        else:
            add_part(mask, low, high)

    held = main + 2 * REM

    def so_terms():
        sums = so_acc[...].reshape(n_shot, n_off, so_acc.shape[1], LANES)
        bins = jnp.sum(sums, axis=0)
        shots = jnp.sum(sums, axis=1)
        lane = lax.broadcasted_iota(jnp.int32, sums.shape, 3)
        both = jnp.where(lane < OFFB_DEV, bins[None], shots[:, None])
        both = both.reshape(so_acc.shape)
        return OMEGA * both[:, :held] / (both[:, held : held + 1] + 1.0)

    def scaled(acc, cnt, cols):
        levels = cnt.shape[0]
        width = cols.stop - cols.start
        low = lower_half((2 * REM, width))

        def main_part(l):
            return acc[l * main : (l + 1) * main, cols] * cnt[l : l + 1, cols]

        def pair_part(pair):
            scale = jnp.where(low, cnt[2 * pair + 1 : 2 * pair + 2, cols], cnt[2 * pair : 2 * pair + 1, cols])
            start = levels * main + 2 * REM * pair
            return acc[start : start + 2 * REM, cols] * scale

        return main_part, pair_part

    rec_cnt[...] = OMEGA / (rec_cnt[...] + 1.0)
    cmp_cnt[...] = OMEGA / (cmp_cnt[...] + 1.0)

    def refresh(x, acc, cnt):
        levels = cnt.shape[0]
        main_part, pair_part = scaled(acc, cnt, slice(0, WIDE))
        parts = [main_part(l) for l in range(levels)] if main else []
        parts += [pair_part(pair) for pair in range(levels // 2)]
        x[...] = jnp.concatenate(parts, axis=0).astype(jnp.bfloat16)

    for _ in range(SWEEPS - 1):
        refresh(rec_x, rec_acc, rec_cnt)
        refresh(cmp_x, cmp_acc, cmp_cnt)
        so = so_terms()
        so_high = so.astype(jnp.bfloat16).astype(jnp.float32)
        so_x[...] = jnp.concatenate([so_high, so - so_high], axis=1).astype(jnp.bfloat16)

        @pl.loop(0, n_dev, unroll=2)
        def _(src):
            add_source(src, False)

    so = so_terms()
    lane8 = lax.broadcasted_iota(jnp.int32, (8, LANES), 1)
    low8 = lower_half((8, LANES))

    def at_zero(values, offset):
        return values if offset == 0 else pltpu.roll(values, LANES - offset, 1)

    for dest in range(n_dev):
        cmp_level, cmp_at = divmod(dest * cmp_rows, WIDE)
        rec_level, rec_at = divmod(dest * rec_rows, WIDE)
        cmp_from, cmp_off = divmod(cmp_at, LANES)
        rec_from, rec_off = divmod(rec_at, LANES)
        cmp_main, cmp_pair = scaled(cmp_acc, cmp_cnt, slice(cmp_from * LANES, (cmp_from + 1) * LANES))
        rec_main, rec_pair = scaled(rec_acc, rec_cnt, slice(rec_from * LANES, (rec_from + 1) * LANES))
        extra = pltpu.roll(so[dest], rec_rows, 1)
        if main:
            ret_stage[dest, :main, :] = at_zero(cmp_main(cmp_level), cmp_off).astype(jnp.bfloat16)
            values = at_zero(rec_main(rec_level), rec_off)
            lane = lax.broadcasted_iota(jnp.int32, values.shape, 1)
            values = jnp.where(lane < rec_rows, values, extra[:main])
            ret_stage[dest, main + 8 :, :] = values.astype(jnp.bfloat16)
        cmp_rest = at_zero(cmp_pair(cmp_level // 2), cmp_off)
        if cmp_level % 2 == 1:
            cmp_rest = pltpu.roll(cmp_rest, REM, 0)
        rec_rest = at_zero(rec_pair(rec_level // 2), rec_off)
        if rec_level % 2 == 0:
            rec_rest = pltpu.roll(rec_rest, REM, 0)
        rec_rest = jnp.where(lane8 < rec_rows, rec_rest, extra[main:])
        ret_stage[dest, main : main + 8, :] = jnp.where(low8, rec_rest, cmp_rest).astype(jnp.bfloat16)

    own = pltpu.make_async_copy(ret_stage.at[me], ret_landed.at[me], own_sems.at[1])
    own.start()
    for mask in (3, 2, 1, 0) if groups == 4 else (0,):

        @pl.loop(1 if mask == 0 else 0, dests)
        def _(step):
            return_copy((my_group ^ mask) * dests + (step + my_place) % dests, me).start()

    drained = {(mask, step) for name, mask, low, high in plan if name == "drain" for step in range(low, high)}
    for mask in range(groups):
        left = [step for step in range(dests) if (mask, step) not in drained]
        if left:
            drain_part(mask, left[0], left[-1] + 1)

    for step in range(1, groups):
        line_copy(step, my_group).wait_send()

    @pl.loop(1, dests)
    def _(step):
        layer_copy((my_place + step) % dests, my_place).wait_send()

    own.wait()

    @pl.loop(1, n_dev)
    def _(step):
        dest = (me + step) % n_dev
        return_copy(dest, me).wait_send()
        return_copy(dest, dest).wait_recv()

    out_ref[...] = ret_landed[...]


def run_terms(traces, ids, owners, sizes, held):
    n_shot, n_off, shot_dev, tr_off, rec_dev, cmp_dev, main = sizes
    n_dev = n_shot * n_off
    tr_dev, samples = traces.shape
    groups = group_count(n_dev)
    dests = n_dev // groups
    rows = dests * (main + REM)
    rec_l = owners[0].shape[0] // WIDE
    cmp_l = owners[2].shape[0] // WIDE
    tables = base_angles(samples, n_dev, held, main)
    vmem = pl.BlockSpec(memory_space=pltpu.VMEM)
    block = (n_dev, 2 * main + 2 * REM, tr_dev // 2)
    ret_block = (n_dev, 2 * main + 8, LANES)
    hot_bytes = n_dev * 2 * WIDE * tr_dev * 2
    kept = n_dev if hot_bytes <= HOT_BYTES else 1
    count = main + REM
    return pl.pallas_call(
        lambda *refs: terms_kernel(sizes, *refs),
        out_shape=jax.ShapeDtypeStruct(ret_block, jnp.bfloat16),
        in_specs=[vmem] * 13,
        out_specs=vmem,
        scratch_shapes=[
            pltpu.VMEM(block, jnp.bfloat16),
            pltpu.VMEM(block, jnp.bfloat16),
            pltpu.VMEM((2 * rows, samples), jnp.bfloat16),
            pltpu.VMEM((8, tr_dev), jnp.int32),
            pltpu.VMEM((ID_ROWS, tr_dev), jnp.float32),
            pltpu.VMEM((dests, groups, ID_ROWS, tr_dev), jnp.bfloat16),
            pltpu.VMEM((2 * rec_l, WIDE), jnp.float32),
            pltpu.VMEM((2 * cmp_l, WIDE), jnp.float32),
            pltpu.VMEM((WIDE, LANES), jnp.bfloat16),
            pltpu.VMEM((kept, 2, WIDE, tr_dev), jnp.bfloat16),
            pltpu.VMEM((rec_l * count, WIDE), jnp.float32),
            pltpu.VMEM((cmp_l * count, WIDE), jnp.float32),
            pltpu.VMEM((rec_l, WIDE), jnp.float32),
            pltpu.VMEM((cmp_l, WIDE), jnp.float32),
            pltpu.VMEM((n_dev, main + 2 * REM + 8, LANES), jnp.float32),
            pltpu.VMEM((rec_l * count, WIDE), jnp.bfloat16),
            pltpu.VMEM((cmp_l * count, WIDE), jnp.bfloat16),
            pltpu.VMEM((n_dev, 2 * (main + 2 * REM), LANES), jnp.bfloat16),
            pltpu.VMEM(ret_block, jnp.bfloat16),
            pltpu.VMEM(ret_block, jnp.bfloat16),
            pltpu.SemaphoreType.DMA((n_dev,)),
            pltpu.SemaphoreType.DMA((n_dev,)),
            pltpu.SemaphoreType.DMA((groups,)),
            pltpu.SemaphoreType.DMA((groups,)),
            pltpu.SemaphoreType.DMA((dests,)),
            pltpu.SemaphoreType.DMA((dests,)),
            pltpu.SemaphoreType.DMA((n_dev,)),
            pltpu.SemaphoreType.DMA((n_dev,)),
            pltpu.SemaphoreType.DMA((2,)),
        ],
        compiler_params=pltpu.CompilerParams(
            vmem_limit_bytes=VMEM_BYTES, collective_id=0, has_side_effects=True
        ),
        name="terms",
    )(traces, *ids, *tables, *owners)


def output_kernel(sizes, held, blocks_ref, source_ref, offset_ref, rec_ref, cmp_ref, joined):
    shot_dev, rec_rows, cmp_rows, main = sizes
    n_dev = blocks_ref.shape[0]
    for src in range(n_dev):
        rows = min(held, NF - src * held)
        if rows > 0:
            block = blocks_ref[src].astype(jnp.float32)
            start = src * held
            joined[start : start + rows, :LANES] = block[:rows]
            first = min(main, rows)
            if first:
                joined[start : start + first, LANES:] = block[main + 8 : main + 8 + first]
            if rows > main:
                joined[start + main : start + rows, LANES:] = block[main + REM : REM + rows]
    turned = joined[...].T
    cmp_ref[...] = turned[:cmp_rows]
    rec_ref[...] = turned[LANES : LANES + rec_rows]
    base = LANES + rec_rows
    offset_ref[...] = turned[base : base + OFFB_DEV]
    source_ref[...] = turned[base + OFFB_DEV : base + OFFB_DEV + shot_dev]


def write_outputs(blocks, sizes, held):
    shot_dev, rec_rows, cmp_rows, main = sizes
    vmem = pl.BlockSpec(memory_space=pltpu.VMEM)
    shape = lambda rows: jax.ShapeDtypeStruct((rows, NF), jnp.float32)
    return pl.pallas_call(
        lambda *refs: output_kernel(sizes, held, *refs),
        out_shape=(shape(shot_dev), shape(OFFB_DEV), shape(rec_rows), shape(cmp_rows)),
        in_specs=[vmem],
        out_specs=(vmem,) * 4,
        scratch_shapes=[pltpu.VMEM((NF, 2 * LANES), jnp.float32)],
        compiler_params=pltpu.CompilerParams(vmem_limit_bytes=VMEM_BYTES),
        name="outputs",
    )(blocks)


def shards(traces, offset_bin, rec_id, cmp_id, rec_owner, rec_slot, cmp_owner, cmp_slot):
    shot_dev, tr_off, samples = traces.shape
    n_shot = lax.axis_size("shot")
    n_off = lax.axis_size("off")
    n_dev = n_shot * n_off
    tr_dev = shot_dev * tr_off
    rec_dev = rec_owner.shape[0] // n_shot
    cmp_dev = cmp_owner.shape[0] // n_shot
    held = up(NF, n_dev) // n_dev
    main = up(max(held - REM, 0), 8)
    blocks = run_terms(
        traces.reshape(tr_dev, samples),
        (offset_bin, rec_id, cmp_id),
        (rec_owner, rec_slot, cmp_owner, cmp_slot),
        (n_shot, n_off, shot_dev, tr_off, rec_dev, cmp_dev, main),
        held,
    )
    sizes = (shot_dev, rec_dev // n_off, cmp_dev // n_off, main)
    return write_outputs(blocks, sizes, held)


def solution(mesh):
    return jax.shard_map(
        shards,
        mesh=mesh,
        in_specs=(
            P("shot", "off", None),
            P("shot", "off"),
            P("shot", "off"),
            P("shot", "off"),
            P(),
            P(),
            P(),
            P(),
        ),
        out_specs=(
            P("shot", None),
            P("off", None),
            P(("shot", "off"), None),
            P(("shot", "off"), None),
        ),
        check_vma=False,
    )
```

```python
import math

import jax
import jax.numpy as jnp
import numpy as np
from jax import lax
from jax.experimental import pallas as pl
from jax.experimental.pallas import tpu as pltpu
from jax.sharding import PartitionSpec as P

NF = 640
OFFB_DEV = 8
SWEEPS = 2
LANES = 128
WIDE = 256
REM = 4
ITEMS = 16
ID_ROWS = 8

OMEGA = 0.35
FLOOR = 0.05
VMEM_BYTES = 60 * 1024 * 1024
HOT_BYTES = 40 * 1024 * 1024


def up(value, unit):
    return -(-value // unit) * unit


def dot_nt(a, b):
    return lax.dot_general(a, b, (((1,), (1,)), ((), ())), preferred_element_type=jnp.float32)


def dot_nn(a, b):
    return lax.dot_general(a, b, (((1,), (0,)), ((), ())), preferred_element_type=jnp.float32)


def group_count(n_dev):
    return 4 if n_dev % 4 == 0 else 1


def base_angles(samples, n_dev, held, main):
    groups = group_count(n_dev)
    dests = n_dev // groups
    rows = dests * (main + REM)
    row = np.arange(groups * rows)
    group, inside = row // rows, row % rows
    in_main = inside < dests * main
    rest = inside - dests * main
    dest = np.where(in_main, inside // max(main, 1), rest // REM)
    place = np.where(in_main, inside % max(main, 1), main + rest % REM)
    freq = ((group * dests + dest) * held + place)[:, None]
    step = 2.0 * math.pi / samples
    coarse = freq * (np.arange(samples // LANES)[None, :] * LANES) % samples * step
    fine = freq * np.arange(LANES)[None, :] % samples * step
    tapers = 0.5 - 0.5 * np.cos((np.arange(samples)[None, :] + 0.5) * step)
    weights = tapers * math.sqrt(8.0 / (3.0 * samples))
    tables = (np.cos(coarse), np.sin(coarse), np.cos(fine), np.sin(fine), weights)
    return tuple(table.astype(np.float32) for table in tables)


def remote(src, dst, send_sem, recv_sem, dest, n_off):
    return pltpu.make_async_remote_copy(
        src_ref=src,
        dst_ref=dst,
        send_sem=send_sem,
        recv_sem=recv_sem,
        device_id=(dest // n_off, dest % n_off),
        device_id_type=pl.DeviceIdType.MESH,
    )


def greet_all(me, n_dev, n_off):
    barrier = pltpu.get_barrier_semaphore()

    @pl.loop(1, n_dev)
    def _(step):
        dest = (me + step) % n_dev
        pl.semaphore_signal(
            barrier,
            inc=1,
            device_id=(dest // n_off, dest % n_off),
            device_id_type=pl.DeviceIdType.MESH,
        )

    return barrier


def lower_half(shape):
    return lax.broadcasted_iota(jnp.int32, shape, 0) >= REM


def fold(values):
    return values + pltpu.roll(values, REM, 0)


def plan_of(groups, dests):
    half = dests // 2
    if groups != 4:
        return [
            ("logs", 0, 0, 0),
            ("layer", 0, 0, 0),
            ("send", 0, 0, dests),
            ("settle", 0, 0, 0),
            ("add", 0, 0, dests),
        ]
    return [
        ("logs", 3, 0, 0),
        ("send", 3, 0, half),
        ("layer", 0, 0, 0),
        ("logs", 2, 0, 0),
        ("send", 3, half, dests),
        ("send", 2, 0, half),
        ("logs", 0, 0, 0),
        ("send", 0, 0, dests),
        ("logs", 1, 0, 0),
        ("settle", 0, 0, 0),
        ("send", 2, half, dests),
        ("add", 0, 0, dests),
        ("send", 1, 0, dests),
        ("add", 3, 0, dests),
        ("add", 1, 0, dests),
        ("add", 2, 0, dests),
    ]


def terms_kernel(
    sizes,
    traces_hbm,
    bin_ref,
    rec_ref,
    cmp_ref,
    ca_ref,
    sa_ref,
    cb_ref,
    sb_ref,
    w_ref,
    rec_owner_ref,
    rec_slot_ref,
    cmp_owner_ref,
    cmp_slot_ref,
    out_ref,
    stage,
    landed,
    even_table,
    odd_table,
    raw,
    id_rows,
    ids,
    rec_tab,
    cmp_tab,
    iota_ref,
    hots,
    rec_acc,
    cmp_acc,
    rec_cnt,
    cmp_cnt,
    so_acc,
    rec_x,
    cmp_x,
    so_x,
    ret_stage,
    ret_landed,
    send_sems,
    recv_sems,
    line_send_sems,
    line_recv_sems,
    layer_send_sems,
    layer_recv_sems,
    ret_send_sems,
    ret_recv_sems,
    own_sems,
    traces_ref,
):
    n_shot, n_off, shot_dev, tr_off, rec_dev, cmp_dev, main = sizes
    n_dev = n_shot * n_off
    groups = group_count(n_dev)
    dests = n_dev // groups
    rows = dests * (main + REM)
    tr_dev, samples = traces_ref.shape
    half = tr_dev // 2
    rec_l = rec_cnt.shape[0]
    cmp_l = cmp_cnt.shape[0]
    rec_rows = rec_dev // n_off
    cmp_rows = cmp_dev // n_off
    keep_hots = hots.shape[0] == n_dev
    me = lax.axis_index("shot") * n_off + lax.axis_index("off")
    my_group = me // dests
    my_place = me % dests
    fetch = pltpu.make_async_copy(traces_hbm, traces_ref, own_sems.at[2])
    fetch.start()
    barrier = greet_all(me, n_dev, n_off)

    def block_copy(dest, slot):
        return remote(
            stage.at[dest], landed.at[slot], send_sems.at[dest], recv_sems.at[slot], dest, n_off
        )

    def line_copy(step, slot):
        block = ids.at[my_place, slot]
        dest = (my_group ^ step) * dests + my_place
        return remote(block, block, line_send_sems.at[step], line_recv_sems.at[step], dest, n_off)

    def layer_copy(place, slot):
        block = ids.at[slot]
        dest = my_group * dests + place
        return remote(block, block, layer_send_sems.at[place], layer_recv_sems.at[slot], dest, n_off)

    def return_copy(dest, slot):
        return remote(
            ret_stage.at[dest],
            ret_landed.at[slot],
            ret_send_sems.at[dest],
            ret_recv_sems.at[slot],
            dest,
            n_off,
        )

    def make_table(group, table):
        base = pl.multiple_of(group * rows, 8)
        cb = cb_ref[pl.ds(base, rows), :]
        sb = sb_ref[pl.ds(base, rows), :]
        ca_all = ca_ref[pl.ds(base, rows), :]
        sa_all = sa_ref[pl.ds(base, rows), :]
        for a in range(samples // LANES):
            cols = slice(a * LANES, (a + 1) * LANES)
            w = w_ref[:, cols]
            ca = ca_all[:, a : a + 1]
            sa = sa_all[:, a : a + 1]
            table[:rows, cols] = (w * (ca * cb - sa * sb)).astype(jnp.bfloat16)
            table[rows:, cols] = (-w * (sa * cb + ca * sb)).astype(jnp.bfloat16)

    def stage_logs(group, turn, later):
        table, spare = (even_table, odd_table) if turn % 2 == 0 else (odd_table, even_table)
        if later is not None:
            make_table(later, spare)
        if turn == 0:
            fetch.wait()
        products = dot_nt(table[...], traces_ref[...])
        real_part = products[:rows]
        imag_part = products[rows:]
        logs = jnp.log(real_part * real_part + imag_part * imag_part + FLOOR)
        first = group * dests
        if main:
            block = logs[: dests * main].reshape(dests, main, tr_dev).astype(jnp.bfloat16)
            stage[pl.ds(first, dests), :main, :] = block[:, :, :half]
            stage[pl.ds(first, dests), main : 2 * main, :] = block[:, :, half:]
        rest = logs[dests * main :]
        low = lower_half((2 * REM, half))
        for pair in range(dests // 2):
            both = rest[2 * REM * pair : 2 * REM * (pair + 1)]
            left, right = both[:, :half], both[:, half:]
            upper = jnp.where(low, pltpu.roll(right, REM, 0), left)
            lower = jnp.where(low, right, pltpu.roll(left, REM, 0))
            stage[first + 2 * pair, 2 * main :, :] = upper.astype(jnp.bfloat16)
            stage[first + 2 * pair + 1, 2 * main :, :] = lower.astype(jnp.bfloat16)

    def one_hot_f32(index):
        row = lax.broadcasted_iota(jnp.int32, (WIDE, index.shape[1]), 0)
        return jnp.where(row == index, 1.0, 0.0).astype(jnp.bfloat16)

    def fill_table(tab, owner_ref, slot_ref, count_dev, levels):
        @pl.loop(0, levels)
        def _(level):
            span = pl.ds(pl.multiple_of(level * WIDE, WIDE), WIDE)
            position = (owner_ref[span] * count_dev + slot_ref[span]).reshape(1, WIDE)
            tab[pl.ds(level, 1), :] = (position // WIDE).astype(jnp.float32)
            tab[pl.ds(levels + level, 1), :] = (position % WIDE).astype(jnp.float32)

    def look_up(index, tab, levels):
        part = dot_nn(tab[...].astype(jnp.bfloat16), one_hot_f32(index % WIDE))
        level = lax.broadcasted_iota(jnp.int32, (levels, index.shape[1]), 0)
        mask = level == index // WIDE
        high = jnp.sum(jnp.where(mask, part[:levels], 0.0), axis=0, keepdims=True)
        low = jnp.sum(jnp.where(mask, part[levels:], 0.0), axis=0, keepdims=True)
        return low, high

    def own_ids():
        fill_table(rec_tab, rec_owner_ref, rec_slot_ref, rec_dev, rec_l)
        fill_table(cmp_tab, cmp_owner_ref, cmp_slot_ref, cmp_dev, cmp_l)
        for shot in range(shot_dev):
            cols = slice(shot * tr_off, (shot + 1) * tr_off)
            raw[0:1, cols] = rec_ref[shot : shot + 1, :]
            raw[1:2, cols] = cmp_ref[shot : shot + 1, :]
            raw[2:3, cols] = bin_ref[shot : shot + 1, :]
        id_rows[...] = jnp.zeros_like(id_rows)
        id_rows[0:1, :], id_rows[1:2, :] = look_up(raw[0:1, :], rec_tab, rec_l)
        id_rows[2:3, :], id_rows[3:4, :] = look_up(raw[1:2, :], cmp_tab, cmp_l)
        id_rows[4:5, :] = (raw[2:3, :] % OFFB_DEV).astype(jnp.float32)
        ids[my_place, my_group] = id_rows[...].astype(jnp.bfloat16)

    def send_line():
        for step in range(1, groups):
            line_copy(step, my_group).start()

    def send_layer():
        for step in range(1, groups):
            line_copy(step, my_group ^ step).wait_recv()

        @pl.loop(1, dests)
        def _(step):
            layer_copy((my_place + step) % dests, my_place).start()

    row_lane = lax.broadcasted_iota(jnp.int32, (WIDE, LANES), 0)
    iota_ref[...] = row_lane.astype(jnp.float32).astype(jnp.bfloat16)
    rec_acc[...] = jnp.zeros_like(rec_acc)
    cmp_acc[...] = jnp.zeros_like(cmp_acc)
    rec_cnt[...] = jnp.zeros_like(rec_cnt)
    cmp_cnt[...] = jnp.zeros_like(cmp_cnt)
    so_acc[...] = jnp.zeros_like(so_acc)

    plan = plan_of(groups, dests)
    log_groups = [my_group ^ mask for name, mask, _, _ in plan if name == "logs"] + [None]
    make_table(log_groups[0], even_table)
    own_ids()
    pl.semaphore_wait(barrier, n_dev - 1)
    send_line()
    chunks = main // 8
    low_full = lower_half((2 * REM, tr_dev))
    low_half = lower_half((2 * REM, half))
    local_shot = lax.broadcasted_iota(jnp.int32, (ITEMS, tr_dev), 1) // tr_off
    item_row = lax.broadcasted_iota(jnp.int32, (ITEMS, tr_dev), 0)
    shot_hot = item_row - OFFB_DEV == local_shot

    row_base = lax.broadcasted_iota(jnp.int32, (16, LANES), 0).astype(jnp.float32)
    row_base = row_base.astype(jnp.bfloat16)

    def make_hot(index):
        column = jnp.broadcast_to(index, (16, tr_dev)).astype(jnp.bfloat16)
        one = jnp.ones((), jnp.bfloat16)
        zero = jnp.zeros((), jnp.bfloat16)
        parts = []
        for i in range(WIDE // 16):
            row = row_base + jnp.full((), 16 * i, jnp.bfloat16)
            pieces = []
            for a in range(tr_dev // LANES):
                piece = column[:, a * LANES : (a + 1) * LANES]
                pieces.append(jnp.where(row == piece, one, zero))
            parts.append(jnp.concatenate(pieces, axis=1))
        return jnp.concatenate(parts, axis=0)

    def level_masks(index, levels):
        level = jnp.broadcast_to(index, (8, tr_dev))
        odd = jnp.where(low_full, level - 1.0, level)
        return (
            lambda l: level == float(l),
            lambda pair: odd == float(2 * pair),
        )

    def spread(mains, rest, index, levels):
        is_level, is_pair = level_masks(index, levels)
        parts = []
        if chunks:
            for l in range(levels):
                mask = is_level(l)
                parts += [jnp.where(mask, part, 0.0) for part in mains]
        for pair in range(levels // 2):
            parts.append(jnp.where(is_pair(pair), rest, 0.0))
        return parts

    def gather(part, index, levels):
        is_level, is_pair = level_masks(index, levels)
        mains = [0.0] * chunks
        if chunks:
            for l in range(levels):
                mask = is_level(l)
                for c in range(chunks):
                    start = l * main + 8 * c
                    mains[c] = mains[c] + jnp.where(mask, part[start : start + 8], 0.0)
        rest = 0.0
        for pair in range(levels // 2):
            start = levels * main + 8 * pair
            rest = rest + jnp.where(is_pair(pair), part[start : start + 8], 0.0)
        return mains, fold(rest)

    def add_source(src, first):
        block = landed[src].astype(jnp.float32)
        rest = block[2 * main :]
        turned = pltpu.roll(rest, REM, 0)
        rest = jnp.concatenate(
            [jnp.where(low_half, turned, rest), jnp.where(low_half, rest, turned)], axis=1
        )
        mains = [
            jnp.concatenate(
                [block[8 * c : 8 * c + 8], block[main + 8 * c : main + 8 * c + 8]], axis=1
            )
            for c in range(chunks)
        ]
        keys = ids[src % dests, src // dests].astype(jnp.float32)
        rec_low, rec_high, cmp_low, cmp_high, bins = (keys[k : k + 1] for k in range(5))
        so_hot = (item_row.astype(jnp.float32) == bins) | shot_hot
        so_hot = jnp.where(so_hot, 1.0, 0.0).astype(jnp.bfloat16)
        if first or not keep_hots:
            rec_hot = make_hot(rec_low)
            cmp_hot = make_hot(cmp_low)
            if keep_hots:
                hots[src, 0] = rec_hot
                hots[src, 1] = cmp_hot
        else:
            rec_hot = hots[src, 0]
            cmp_hot = hots[src, 1]
        if not first:
            so_part = dot_nn(so_x[src][:, :ITEMS], so_hot)
            held = main + 2 * REM
            so_part = so_part[:held] + so_part[held:]
            rec_mains, rec_rest = gather(dot_nn(rec_x[...], rec_hot), rec_high, rec_l)
            cmp_mains, cmp_rest = gather(dot_nn(cmp_x[...], cmp_hot), cmp_high, cmp_l)
            for c in range(chunks):
                mains[c] = mains[c] - so_part[8 * c : 8 * c + 8] - rec_mains[c] - cmp_mains[c]
            rest = rest - so_part[main:] - rec_rest - cmp_rest
        rec_parts = spread(mains, rest, rec_high, rec_l)
        cmp_parts = spread(mains, rest, cmp_high, cmp_l)
        so_parts = mains + [rest]
        if first:
            for parts, index, levels in ((rec_parts, rec_high, rec_l), (cmp_parts, cmp_high, cmp_l)):
                level = lax.broadcasted_iota(jnp.int32, (levels, tr_dev), 0)
                parts.append(jnp.where(level.astype(jnp.float32) == index, 1.0, 0.0))
            so_parts = so_parts + [jnp.ones((8, tr_dev), jnp.float32)]
        join = lambda parts: jnp.concatenate(parts, axis=0).astype(jnp.bfloat16)
        rec_sum = dot_nt(join(rec_parts), rec_hot)
        cmp_sum = dot_nt(join(cmp_parts), cmp_hot)
        so_sum = dot_nt(join(so_parts), so_hot)
        rec_acc[...] += rec_sum[: rec_acc.shape[0]]
        cmp_acc[...] += cmp_sum[: cmp_acc.shape[0]]
        if first:
            rec_cnt[...] += rec_sum[rec_acc.shape[0] :]
            cmp_cnt[...] += cmp_sum[cmp_acc.shape[0] :]
            so_acc[src, :, 0:ITEMS] = so_sum
        else:
            so_acc[src, 0 : main + 2 * REM, 0:ITEMS] += so_sum

    def send_part(mask, low, high):
        @pl.loop(max(low, 1) if mask == 0 else low, high)
        def _(step):
            block_copy((my_group ^ mask) * dests + (step + my_place) % dests, me).start()

    def drain_part(mask, low, high):
        @pl.loop(max(low, 1) if mask == 0 else low, high)
        def _(step):
            block_copy((my_group ^ mask) * dests + (step + my_place) % dests, me).wait_send()

    def add_part(mask, low, high):
        @pl.loop(low, high, unroll=4)
        def _(step):
            src = (my_group ^ mask) * dests + (my_place + dests - step) % dests
            if mask == 0 and low == 0:

                @pl.when(step > 0)
                def _():
                    block_copy(src, src).wait_recv()

            else:
                block_copy(src, src).wait_recv()
            add_source(src, True)

    def settle_own():
        own = pltpu.make_async_copy(stage.at[me], landed.at[me], own_sems.at[0])
        own.start()
        own.wait()

        @pl.loop(1, dests)
        def _(step):
            place = (my_place + dests - step) % dests
            layer_copy(place, place).wait_recv()

    turn = 0
    for name, mask, low, high in plan:
        if name == "logs":
            stage_logs(my_group ^ mask, turn, log_groups[turn + 1])
            turn += 1
        elif name == "layer":
            send_layer()
        elif name == "send":
            send_part(mask, low, high)
        elif name == "drain":
            drain_part(mask, low, high)
        elif name == "settle":
            settle_own()
        else:
            add_part(mask, low, high)

    held = main + 2 * REM

    def so_terms():
        sums = so_acc[...].reshape(n_shot, n_off, so_acc.shape[1], LANES)
        bins = jnp.sum(sums, axis=0)
        shots = jnp.sum(sums, axis=1)
        lane = lax.broadcasted_iota(jnp.int32, sums.shape, 3)
        both = jnp.where(lane < OFFB_DEV, bins[None], shots[:, None])
        both = both.reshape(so_acc.shape)
        return OMEGA * both[:, :held] / (both[:, held : held + 1] + 1.0)

    def scaled(acc, cnt, cols):
        levels = cnt.shape[0]
        width = cols.stop - cols.start
        low = lower_half((2 * REM, width))

        def main_part(l):
            return acc[l * main : (l + 1) * main, cols] * cnt[l : l + 1, cols]

        def pair_part(pair):
            scale = jnp.where(low, cnt[2 * pair + 1 : 2 * pair + 2, cols], cnt[2 * pair : 2 * pair + 1, cols])
            start = levels * main + 2 * REM * pair
            return acc[start : start + 2 * REM, cols] * scale

        return main_part, pair_part

    rec_cnt[...] = OMEGA / (rec_cnt[...] + 1.0)
    cmp_cnt[...] = OMEGA / (cmp_cnt[...] + 1.0)

    def refresh(x, acc, cnt):
        levels = cnt.shape[0]
        main_part, pair_part = scaled(acc, cnt, slice(0, WIDE))
        parts = [main_part(l) for l in range(levels)] if main else []
        parts += [pair_part(pair) for pair in range(levels // 2)]
        x[...] = jnp.concatenate(parts, axis=0).astype(jnp.bfloat16)

    for _ in range(SWEEPS - 1):
        refresh(rec_x, rec_acc, rec_cnt)
        refresh(cmp_x, cmp_acc, cmp_cnt)
        so = so_terms()
        so_high = so.astype(jnp.bfloat16).astype(jnp.float32)
        so_x[...] = jnp.concatenate([so_high, so - so_high], axis=1).astype(jnp.bfloat16)

        @pl.loop(0, n_dev, unroll=4)
        def _(src):
            add_source(src, False)

    so = so_terms()
    lane8 = lax.broadcasted_iota(jnp.int32, (8, LANES), 1)
    low8 = lower_half((8, LANES))

    def at_zero(values, offset):
        return values if offset == 0 else pltpu.roll(values, LANES - offset, 1)

    for dest in range(n_dev):
        cmp_level, cmp_at = divmod(dest * cmp_rows, WIDE)
        rec_level, rec_at = divmod(dest * rec_rows, WIDE)
        cmp_from, cmp_off = divmod(cmp_at, LANES)
        rec_from, rec_off = divmod(rec_at, LANES)
        cmp_main, cmp_pair = scaled(cmp_acc, cmp_cnt, slice(cmp_from * LANES, (cmp_from + 1) * LANES))
        rec_main, rec_pair = scaled(rec_acc, rec_cnt, slice(rec_from * LANES, (rec_from + 1) * LANES))
        extra = pltpu.roll(so[dest], rec_rows, 1)
        if main:
            ret_stage[dest, :main, :] = at_zero(cmp_main(cmp_level), cmp_off).astype(jnp.bfloat16)
            values = at_zero(rec_main(rec_level), rec_off)
            lane = lax.broadcasted_iota(jnp.int32, values.shape, 1)
            values = jnp.where(lane < rec_rows, values, extra[:main])
            ret_stage[dest, main + 8 :, :] = values.astype(jnp.bfloat16)
        cmp_rest = at_zero(cmp_pair(cmp_level // 2), cmp_off)
        if cmp_level % 2 == 1:
            cmp_rest = pltpu.roll(cmp_rest, REM, 0)
        rec_rest = at_zero(rec_pair(rec_level // 2), rec_off)
        if rec_level % 2 == 0:
            rec_rest = pltpu.roll(rec_rest, REM, 0)
        rec_rest = jnp.where(lane8 < rec_rows, rec_rest, extra[main:])
        ret_stage[dest, main : main + 8, :] = jnp.where(low8, rec_rest, cmp_rest).astype(jnp.bfloat16)

    own = pltpu.make_async_copy(ret_stage.at[me], ret_landed.at[me], own_sems.at[1])
    own.start()
    for mask in (3, 2, 1, 0) if groups == 4 else (0,):

        @pl.loop(1 if mask == 0 else 0, dests)
        def _(step):
            return_copy((my_group ^ mask) * dests + (step + my_place) % dests, me).start()

    drained = {(mask, step) for name, mask, low, high in plan if name == "drain" for step in range(low, high)}
    for mask in range(groups):
        left = [step for step in range(dests) if (mask, step) not in drained]
        if left:
            drain_part(mask, left[0], left[-1] + 1)

    for step in range(1, groups):
        line_copy(step, my_group).wait_send()

    @pl.loop(1, dests)
    def _(step):
        layer_copy((my_place + step) % dests, my_place).wait_send()

    own.wait()

    @pl.loop(1, n_dev)
    def _(step):
        dest = (me + step) % n_dev
        return_copy(dest, me).wait_send()
        return_copy(dest, dest).wait_recv()

    out_ref[...] = ret_landed[...]


def run_terms(traces, ids, owners, sizes, held):
    n_shot, n_off, shot_dev, tr_off, rec_dev, cmp_dev, main = sizes
    n_dev = n_shot * n_off
    tr_dev, samples = traces.shape
    groups = group_count(n_dev)
    dests = n_dev // groups
    rows = dests * (main + REM)
    rec_l = owners[0].shape[0] // WIDE
    cmp_l = owners[2].shape[0] // WIDE
    tables = base_angles(samples, n_dev, held, main)
    vmem = pl.BlockSpec(memory_space=pltpu.VMEM)
    block = (n_dev, 2 * main + 2 * REM, tr_dev // 2)
    ret_block = (n_dev, 2 * main + 8, LANES)
    hot_bytes = n_dev * 2 * WIDE * tr_dev * 2
    kept = n_dev if hot_bytes <= HOT_BYTES else 1
    count = main + REM
    return pl.pallas_call(
        lambda *refs: terms_kernel(sizes, *refs),
        out_shape=jax.ShapeDtypeStruct(ret_block, jnp.bfloat16),
        in_specs=[pl.BlockSpec(memory_space=pl.ANY)] + [vmem] * 12,
        out_specs=vmem,
        scratch_shapes=[
            pltpu.VMEM(block, jnp.bfloat16),
            pltpu.VMEM(block, jnp.bfloat16),
            pltpu.VMEM((2 * rows, samples), jnp.bfloat16),
            pltpu.VMEM((2 * rows, samples), jnp.bfloat16),
            pltpu.VMEM((8, tr_dev), jnp.int32),
            pltpu.VMEM((ID_ROWS, tr_dev), jnp.float32),
            pltpu.VMEM((dests, groups, ID_ROWS, tr_dev), jnp.bfloat16),
            pltpu.VMEM((2 * rec_l, WIDE), jnp.float32),
            pltpu.VMEM((2 * cmp_l, WIDE), jnp.float32),
            pltpu.VMEM((WIDE, LANES), jnp.bfloat16),
            pltpu.VMEM((kept, 2, WIDE, tr_dev), jnp.bfloat16),
            pltpu.VMEM((rec_l * count, WIDE), jnp.float32),
            pltpu.VMEM((cmp_l * count, WIDE), jnp.float32),
            pltpu.VMEM((rec_l, WIDE), jnp.float32),
            pltpu.VMEM((cmp_l, WIDE), jnp.float32),
            pltpu.VMEM((n_dev, main + 2 * REM + 8, LANES), jnp.float32),
            pltpu.VMEM((rec_l * count, WIDE), jnp.bfloat16),
            pltpu.VMEM((cmp_l * count, WIDE), jnp.bfloat16),
            pltpu.VMEM((n_dev, 2 * (main + 2 * REM), LANES), jnp.bfloat16),
            pltpu.VMEM(ret_block, jnp.bfloat16),
            pltpu.VMEM(ret_block, jnp.bfloat16),
            pltpu.SemaphoreType.DMA((n_dev,)),
            pltpu.SemaphoreType.DMA((n_dev,)),
            pltpu.SemaphoreType.DMA((groups,)),
            pltpu.SemaphoreType.DMA((groups,)),
            pltpu.SemaphoreType.DMA((dests,)),
            pltpu.SemaphoreType.DMA((dests,)),
            pltpu.SemaphoreType.DMA((n_dev,)),
            pltpu.SemaphoreType.DMA((n_dev,)),
            pltpu.SemaphoreType.DMA((3,)),
            pltpu.VMEM((tr_dev, samples), jnp.bfloat16),
        ],
        compiler_params=pltpu.CompilerParams(
            vmem_limit_bytes=VMEM_BYTES, collective_id=0, has_side_effects=True
        ),
        name="terms",
    )(traces, *ids, *tables, *owners)


def output_kernel(sizes, held, blocks_ref, source_ref, offset_ref, rec_ref, cmp_ref, joined):
    shot_dev, rec_rows, cmp_rows, main = sizes
    n_dev = blocks_ref.shape[0]
    for src in range(n_dev):
        rows = min(held, NF - src * held)
        if rows > 0:
            block = blocks_ref[src].astype(jnp.float32)
            start = src * held
            joined[start : start + rows, :LANES] = block[:rows]
            first = min(main, rows)
            if first:
                joined[start : start + first, LANES:] = block[main + 8 : main + 8 + first]
            if rows > main:
                joined[start + main : start + rows, LANES:] = block[main + REM : REM + rows]
    turned = joined[...].T
    cmp_ref[...] = turned[:cmp_rows]
    rec_ref[...] = turned[LANES : LANES + rec_rows]
    base = LANES + rec_rows
    offset_ref[...] = turned[base : base + OFFB_DEV]
    source_ref[...] = turned[base + OFFB_DEV : base + OFFB_DEV + shot_dev]


def write_outputs(blocks, sizes, held):
    shot_dev, rec_rows, cmp_rows, main = sizes
    vmem = pl.BlockSpec(memory_space=pltpu.VMEM)
    shape = lambda rows: jax.ShapeDtypeStruct((rows, NF), jnp.float32)
    return pl.pallas_call(
        lambda *refs: output_kernel(sizes, held, *refs),
        out_shape=(shape(shot_dev), shape(OFFB_DEV), shape(rec_rows), shape(cmp_rows)),
        in_specs=[vmem],
        out_specs=(vmem,) * 4,
        scratch_shapes=[pltpu.VMEM((NF, 2 * LANES), jnp.float32)],
        compiler_params=pltpu.CompilerParams(vmem_limit_bytes=VMEM_BYTES),
        name="outputs",
    )(blocks)


def shards(traces, offset_bin, rec_id, cmp_id, rec_owner, rec_slot, cmp_owner, cmp_slot):
    shot_dev, tr_off, samples = traces.shape
    n_shot = lax.axis_size("shot")
    n_off = lax.axis_size("off")
    n_dev = n_shot * n_off
    tr_dev = shot_dev * tr_off
    rec_dev = rec_owner.shape[0] // n_shot
    cmp_dev = cmp_owner.shape[0] // n_shot
    held = up(NF, n_dev) // n_dev
    main = up(max(held - REM, 0), 8)
    blocks = run_terms(
        traces.reshape(tr_dev, samples),
        (offset_bin, rec_id, cmp_id),
        (rec_owner, rec_slot, cmp_owner, cmp_slot),
        (n_shot, n_off, shot_dev, tr_off, rec_dev, cmp_dev, main),
        held,
    )
    sizes = (shot_dev, rec_dev // n_off, cmp_dev // n_off, main)
    return write_outputs(blocks, sizes, held)


def solution(mesh):
    return jax.shard_map(
        shards,
        mesh=mesh,
        in_specs=(
            P("shot", "off", None),
            P("shot", "off"),
            P("shot", "off"),
            P("shot", "off"),
            P(),
            P(),
            P(),
            P(),
        ),
        out_specs=(
            P("shot", None),
            P("off", None),
            P(("shot", "off"), None),
            P(("shot", "off"), None),
        ),
        check_vma=False,
    )
```
